256 devices in a mesh: leaf: 64 (over z, x, core), rep: 4 (over y).
Axes of the slice: x: 4, y: 4, z: 8, core: 2. Of those that a mesh axis runs over, the one named last changes fastest.
Arguments:
- leaf_blocks: float32 [65536, 1024], P('leaf'), as said below
- generators: float32 [6, 128, 65536], P(None, 'rep', 'leaf'), may hold values from -0.5 to 0.5
- rhs: float32 [128, 65536], P('rep', 'leaf'), may hold values from -6 to 6
- order: int32 [64, 1024], P('leaf'), may hold values from 0 to 1023, each once within a row
- ranks: int32 [6, 64], P(None, 'leaf'), may hold values from 32 to 128, as said below
Outputs:
- solution: float32 [128, 65536], P('rep', 'leaf')
- determinants: float32 [7], replicated
The draws below stay inside these ranges and needn't reach their ends.
Inputs may be any that keep to these rules, and one draw needn't show every extreme that they name: `leaf_blocks`: each block of 1024 rows is a symmetric positive definite leaf covariance block. ranks[k, i] is equal for all leaves i of one depth-k node (equal i // 2**(k+1)); every level has a node of full rank 128. Each row of order is a permutation of the 1024 positions.
All inputs are finite; a program needn't handle non-finite values.
Results may differ from the reference program's by a relative error of at most 0.0003.
Values sent between devices are 32-bit elements; how exact they have to be, the bound alone decides.
A program may use at most 128 MiB of HBM per device.

```python
import jax
import jax.numpy as jnp
from jax import lax

M = 1024
R = 128
NRHS = 128
LEAVES = 64
LEVELS = 6
N = 65536


length_scale = 0.1


noise_weight = 0.25


def matern_block(key, leaf):
    point_key, noise_key, nugget_key = jax.random.split(jax.random.fold_in(key, leaf + 101), 3)
    points = jax.random.uniform(point_key, (M, 2), jnp.float32, 0.0, 1.0)
    nugget = jax.random.uniform(nugget_key, (M,), jnp.float32, 0.4, 1.0)
    delta_x = points[:, 0][:, None] - points[:, 0][None, :]
    delta_y = points[:, 1][:, None] - points[:, 1][None, :]
    scaled = jnp.sqrt(3.0) * jnp.sqrt(delta_x * delta_x + delta_y * delta_y) / length_scale
    kernel = (1.0 + scaled) * jnp.exp(-scaled)
    uniform_draw = jax.random.uniform(noise_key, (M, M), jnp.float32, -1.0, 1.0)
    noise = 0.5 * (uniform_draw + uniform_draw.T) * (noise_weight / jnp.sqrt(jnp.float32(M)))
    identity = jnp.eye(M, dtype=jnp.float32)
    block = kernel + noise * (1.0 - identity) + identity * nugget[:, None]
    growth = 9.0 ** (leaf.astype(jnp.float32) / max(LEAVES - 1, 1))
    return block * growth


def draw_leaf_blocks(key, part):
    blocks = lax.map(lambda leaf: matern_block(key, leaf), jnp.arange(LEAVES, dtype=jnp.int32))
    return blocks.reshape(LEAVES * M, M)


def draw_ranks(key, part):
    leaf_index = jnp.arange(LEAVES, dtype=jnp.int32)
    per_level = []
    for depth in range(LEVELS):
        node_key, pick_key = jax.random.split(jax.random.fold_in(key, depth + 11))
        nodes = LEAVES // 2 ** (depth + 1)
        per_node = jax.random.randint(node_key, (nodes,), R // 4, R + 1, dtype=jnp.int32)
        chosen = jax.random.randint(pick_key, (), 0, nodes, dtype=jnp.int32)
        per_node = jnp.where(jnp.arange(nodes, dtype=jnp.int32) == chosen, R, per_node)
        per_level.append(per_node[leaf_index // 2 ** (depth + 1)])
    return jnp.stack(per_level).astype(jnp.int32)


def level_of(key, shape, cuts, least, high):
    def one(axis_at, blocks):
        steps = jax.random.uniform(jax.random.fold_in(jax.random.fold_in(key, 6), axis_at), (blocks,), jnp.float32, least / len(cuts), high / len(cuts))
        return jnp.repeat(jnp.exp(steps), shape[axis_at] // blocks).reshape((-1,) + (1,) * (len(shape) - axis_at - 1))

    gain = one(*cuts[0])
    for cut in cuts[1:]:
        gain = gain * one(*cut)
    return gain


def centred(own_key, extent, deviation, reach, pieces=(), kind=jnp.bfloat16):
    drawn = jax.random.normal(own_key, extent, jnp.float32) * deviation
    if len(pieces) > 0:
        drawn = level_of(own_key, extent, pieces, -0.22, 0.18) * drawn
    return jnp.clip(drawn, min=-reach, max=reach).astype(kind)


def setup_inputs(seed: int = 0) -> dict:
    arg_keys = jax.random.split(jax.random.key(seed), 6)
    leaf_blocks = draw_leaf_blocks(jax.random.fold_in(arg_keys[5], 71), 0)
    generators = centred(arg_keys[1], (LEVELS, R, N), R ** -0.5, 0.5, ((1, 4), (2, 64)), jnp.float32)
    rhs = centred(arg_keys[2], (NRHS, N), 1.0, 6.0, ((0, 4), (1, 64)), jnp.float32)
    order = jax.vmap(lambda own: jax.random.permutation(own, M))(jax.random.split(arg_keys[3], LEAVES)).reshape((LEAVES, M)).astype(jnp.int32)
    ranks = draw_ranks(jax.random.fold_in(arg_keys[5], 71), 0)
    return dict(leaf_blocks=leaf_blocks, generators=generators, rhs=rhs, order=order, ranks=ranks)


HIGHEST = lax.Precision.HIGHEST

def product(left, right):
    return jnp.dot(left.astype(jnp.float32), right.astype(jnp.float32), precision=HIGHEST, preferred_element_type=jnp.float32)

def solve_with(factor, values):
    return jax.scipy.linalg.cho_solve((factor, True), values)

def log_det(factor, count):
    return 2.0 * jnp.sum(jnp.log(jnp.diagonal(factor))) / count

def leaf_factor(inputs):
    block, stacked, tree_rhs = inputs
    factor = jnp.linalg.cholesky(block)
    gram_block = product(stacked, solve_with(factor, stacked.T))
    cross_block = product(stacked, solve_with(factor, tree_rhs.T))
    return (factor, jnp.concatenate([gram_block, cross_block], axis=1), log_det(factor, M))

def reference(leaf_blocks, generators, rhs, order, ranks):
    blocks = leaf_blocks.reshape(LEAVES, M, M)
    rank_index = lax.broadcasted_iota(jnp.int32, (LEVELS, R, LEAVES), 1)
    live = rank_index < ranks[:, None, :]
    masked = jnp.where(live[:, :, :, None], generators.reshape(LEVELS, R, LEAVES, M), 0.0)
    stacked = jnp.transpose(masked, (2, 0, 1, 3)).reshape(LEAVES, LEVELS * R, M)
    sensor = jnp.transpose(rhs.reshape(NRHS, LEAVES, M), (1, 0, 2))
    tree_rhs = jax.vmap(lambda values, index: jnp.take(values, index, axis=1))(sensor, order)
    factors, reduced, leaf_dets = lax.map(leaf_factor, (blocks, stacked, tree_rhs))
    batched_solve = jax.vmap(solve_with)
    identity = jnp.eye(R, dtype=jnp.float32)
    results = [jnp.mean(leaf_dets)]
    pivots = []
    for depth in range(LEVELS):
        merged = reduced[0::2] + reduced[1::2]
        pivot_rows = merged[:, :R]
        pivot_factor = jnp.linalg.cholesky(identity[None] + pivot_rows[:, :, :R])
        node_dets = 2.0 * jnp.sum(jnp.log(jnp.diagonal(pivot_factor, axis1=1, axis2=2)), axis=1) / R
        results.append(jnp.mean(node_dets))
        pivot_right = pivot_rows[:, :, R:]
        pivots.append((pivot_factor, pivot_right))
        lower_rows = merged[:, R:]
        reduced = lower_rows[:, :, R:] - jnp.einsum('nab,nbc->nac', lower_rows[:, :, :R], batched_solve(pivot_factor, pivot_right), precision=HIGHEST)
    coeffs = [None] * LEVELS
    for depth in reversed(range(LEVELS)):
        pivot_factor, pivot_right = pivots[depth]
        after = LEVELS - depth - 1
        target = pivot_right[:, :, after * R:]
        for ancestor in range(depth + 1, LEVELS):
            offset = (ancestor - depth - 1) * R
            parent = jnp.repeat(coeffs[ancestor], 2 ** (ancestor - depth), axis=0)
            target = target - jnp.einsum('nab,nbc->nac', pivot_right[:, :, offset:offset + R], parent, precision=HIGHEST)
        coeffs[depth] = batched_solve(pivot_factor, target)
    correction = jnp.transpose(tree_rhs, (0, 2, 1))
    for depth in range(LEVELS):
        per_leaf = jnp.repeat(coeffs[depth], 2 ** (depth + 1), axis=0)
        correction = correction - jnp.einsum('prm,prc->pmc', stacked[:, depth * R:(depth + 1) * R], per_leaf, precision=HIGHEST)
    solution_tree = batched_solve(factors, correction)
    placed = jax.vmap(lambda values, index: jnp.zeros_like(values).at[:, index].set(values))(jnp.transpose(solution_tree, (0, 2, 1)), order)
    solution = jnp.transpose(placed, (1, 0, 2)).reshape(NRHS, LEAVES * M)
    return (solution, jnp.stack(results))
```

```python
import functools

import jax
import jax.numpy as jnp
from jax import lax
from jax.experimental import pallas as pl
from jax.experimental.pallas import tpu as pltpu
from jax.sharding import PartitionSpec as P

HIGHEST = lax.Precision.HIGHEST
B = 128
T = 8


def swapped(value, axis, bit):
    mask = 2**bit
    pairs = [(source, source ^ mask) for source in range(lax.axis_size(axis))]
    return lax.ppermute(value, axis, pairs)


def dot_nn(left, right):
    return jnp.dot(left, right, precision=HIGHEST, preferred_element_type=jnp.float32)


def dot_nt(left, right):
    return lax.dot_general(
        left, right, (((1,), (1,)), ((), ())), precision=HIGHEST, preferred_element_type=jnp.float32
    )


def spread(row):
    return jnp.broadcast_to(row, (T, B))


def eliminate(s_ref, t_ref):
    sub = lax.broadcasted_iota(jnp.int32, (T, B), 0)
    rows = lax.broadcasted_iota(jnp.int32, (B, B), 0)
    lanes = lax.broadcasted_iota(jnp.int32, (B, B), 1)
    t_ref[...] = jnp.where(rows == lanes, 1.0, 0.0).astype(jnp.float32)
    logs = jnp.zeros((T, B), jnp.float32)
    for tile in range(B // T):
        lo = tile * T
        p = s_ref[lo : lo + T, :]
        q = t_ref[lo : lo + T, :]
        cols = [spread(p[:, lo + j : lo + j + 1]) for j in range(T)]
        diag = jnp.zeros((T, B), jnp.float32)
        for j in range(T):
            pivot = spread(cols[j][j : j + 1])
            diag = jnp.where(sub == j, pivot, diag)
            if j < T - 1:
                factor = jnp.where(sub > j, cols[j] * (1.0 / pivot), 0.0)
                for other in range(j + 1, T):
                    cols[other] = cols[other] - factor * spread(cols[other][j : j + 1])
                p = p - factor * spread(p[j : j + 1])
                q = q - factor * spread(q[j : j + 1])
        logs = logs + jnp.log(diag)
        t_ref[lo : lo + T, :] = q * lax.rsqrt(diag)
        if lo + T < B:
            inverse = 1.0 / diag
            p = p * inverse
            q = q * inverse
            for j in range(T - 1, 0, -1):
                factor = jnp.where(sub < j, cols[j] * inverse, 0.0)
                p = p - factor * spread(p[j : j + 1])
                q = q - factor * spread(q[j : j + 1])
            p_rows = [spread(p[j : j + 1]) for j in range(T)]
            q_rows = [spread(q[j : j + 1]) for j in range(T)]
            for below in range(tile + 1, B // T):
                at = below * T
                s_tile = s_ref[at : at + T, :]
                t_tile = t_ref[at : at + T, :]
                s_sum = jnp.zeros((T, B), jnp.float32)
                t_sum = jnp.zeros((T, B), jnp.float32)
                for j in range(T):
                    column = spread(s_tile[:, lo + j : lo + j + 1])
                    s_sum = s_sum + column * p_rows[j]
                    t_sum = t_sum + column * q_rows[j]
                s_ref[at : at + T, :] = s_tile - s_sum
                t_ref[at : at + T, :] = t_tile - t_sum
    return logs


def factor_kernel(d_ref, l_ref, inv_ref, log_ref, s_ref, t_ref):
    points = d_ref.shape[0]
    blocks = points // B
    l_ref[...] = d_ref[...]

    def panel(j, logs):
        at = pl.multiple_of(j * B, B)
        s_ref[...] = l_ref[pl.ds(at, B), pl.ds(at, B)]
        logs = logs + eliminate(s_ref, t_ref)
        inv_ref[pl.ds(at, B), :] = t_ref[...]
        for own in range(blocks - 1):
            lo = (own + 1) * B

            @pl.when(j == own)
            def _():
                @pl.loop(own + 1, blocks)
                def _(r):
                    row = pl.multiple_of(r * B, B)
                    l_ref[pl.ds(row, B), own * B : lo] = dot_nt(
                        l_ref[pl.ds(row, B), own * B : lo], t_ref[...]
                    )

                @pl.loop(own + 1, blocks)
                def _(r):
                    row = pl.multiple_of(r * B, B)
                    l_ref[pl.ds(row, B), lo:] = l_ref[pl.ds(row, B), lo:] - dot_nt(
                        l_ref[pl.ds(row, B), own * B : lo], l_ref[lo:, own * B : lo]
                    )

        return logs

    logs = lax.fori_loop(0, blocks, panel, jnp.zeros((T, B), jnp.float32))
    log_ref[...] = jnp.broadcast_to(jnp.sum(logs, axis=0, keepdims=True), (T, B))


def leaf_kernel(a_ref, r_ref, order_ref, l_ref, inv_ref, log_ref, x_ref, red_ref):
    width, points = a_ref.shape
    count = r_ref.shape[0]
    blocks = points // B
    sensor = lax.broadcasted_iota(jnp.int32, (points, B), 0)
    for j in range(blocks):
        lo = j * B
        pick = jnp.where(sensor == order_ref[0:1, lo : lo + B], 1.0, 0.0).astype(jnp.float32)
        x_ref[width:, lo : lo + B] = dot_nn(r_ref[...], pick)
        x_ref[:width, lo : lo + B] = a_ref[:, lo : lo + B]
    step = (width + count) // 4
    for j in range(blocks):
        lo = j * B

        @pl.loop(0, 4)
        def _(r):
            rows = pl.ds(pl.multiple_of(r * step, T), step)
            value = x_ref[rows, lo : lo + B]
            if j > 0:
                value = value - dot_nt(x_ref[rows, :lo], l_ref[lo : lo + B, :lo])
            x_ref[rows, lo : lo + B] = dot_nt(value, inv_ref[lo : lo + B, :])

    @pl.loop(0, 4)
    def _(r):
        rows = pl.ds(pl.multiple_of(r * step, T), step)
        red_ref[rows, :] = dot_nt(x_ref[rows, :], x_ref[:width, :])

    lane = lax.broadcasted_iota(jnp.int32, (T, width), 1)
    red_ref[width + count :, :] = jnp.where(lane == 0, log_ref[0:1, 0:1], 0.0)


def level_kernel(depth, count, own_ref, other_ref, inv_ref, y_ref, *rest):
    out_ref, s_ref, t_ref = rest
    width = own_ref.shape[1]
    left = width - B
    rows = lax.broadcasted_iota(jnp.int32, (B, B), 0)
    lanes = lax.broadcasted_iota(jnp.int32, (B, B), 1)
    eye = jnp.where(rows == lanes, 1.0, 0.0).astype(jnp.float32)
    s_ref[...] = eye + (own_ref[:B, :B] + other_ref[:B, :B])
    logs = eliminate(s_ref, t_ref)
    total = jnp.sum(logs, axis=0, keepdims=True)
    inv_ref[...] = t_ref[...]
    end = width + count
    y_ref[...] = dot_nt(own_ref[B:end, :B] + other_ref[B:end, :B], t_ref[...])
    sums = own_ref[end:, :B] + other_ref[end:, :B]
    lane = lax.broadcasted_iota(jnp.int32, (T, B), 1)
    sums = jnp.where(lane == depth + 1, total, sums)
    if left == 0:
        out_ref[...] = sums
        return
    for lo in range(0, left + count, B):
        hi = min(lo + B, left + count)
        out_ref[lo:hi, :] = (
            own_ref[B + lo : B + hi, B:] + other_ref[B + lo : B + hi, B:]
        ) - dot_nt(y_ref[lo:hi, :], y_ref[:left, :])
    out_ref[left + count :, :] = jnp.zeros((T, left), jnp.float32)
    out_ref[left + count :, :B] = sums


def back_kernel(levels, *refs):
    invs = refs[:levels]
    ys = refs[levels : 2 * levels]
    x_ref, l_ref, inv_ref, order_ref, out_ref, c_ref, z_ref = refs[2 * levels :]
    count, points = out_ref.shape
    width = levels * B
    blocks = points // B
    for depth in reversed(range(levels)):
        left = (levels - depth - 1) * B
        target = ys[depth][left:, :]
        lo = depth * B
        if left > 0:
            target = target - dot_nn(c_ref[:, lo + B :], ys[depth][:left, :])
        c_ref[:, lo : lo + B] = dot_nn(target, invs[depth][...])
    for j in range(blocks):
        lo = j * B
        z_ref[:, lo : lo + B] = x_ref[width:, lo : lo + B] - dot_nn(
            c_ref[...], x_ref[:width, lo : lo + B]
        )
    for j in reversed(range(blocks)):
        lo = j * B
        value = z_ref[:, lo : lo + B]
        if j < blocks - 1:
            value = value - dot_nn(z_ref[:, lo + B :], l_ref[lo + B :, lo : lo + B])
        z_ref[:, lo : lo + B] = dot_nn(value, inv_ref[lo : lo + B, :])
    sensor = lax.broadcasted_iota(jnp.int32, (points, B), 0)
    for j in range(blocks):
        lo = j * B
        pick = jnp.where(sensor == order_ref[0:1, lo : lo + B], 1.0, 0.0).astype(jnp.float32)
        part = dot_nt(z_ref[:, lo : lo + B], pick)
        out_ref[...] = part if j == 0 else out_ref[...] + part


def call(kernel, name, outs, scratch, *operands):
    return pl.pallas_call(
        kernel,
        name=name,
        out_shape=[jax.ShapeDtypeStruct(shape, jnp.float32) for shape in outs],
        in_specs=[pl.BlockSpec(memory_space=pltpu.VMEM)] * len(operands),
        out_specs=[pl.BlockSpec(memory_space=pltpu.VMEM)] * len(outs),
        scratch_shapes=[pltpu.VMEM(shape, jnp.float32) for shape in scratch],
        compiler_params=pltpu.CompilerParams(vmem_limit_bytes=48 * 2**20),
    )(*operands)


def shards(leaf_blocks, generators, rhs, order, ranks):
    levels, quarter, points = generators.shape
    count = rhs.shape[0]
    replica = lax.axis_index("rep")
    rank_index = lax.broadcasted_iota(jnp.int32, (levels, quarter, 1), 1) + replica * quarter
    masked = jnp.where(rank_index < ranks[:, :, None], generators, 0.0)
    gathered = lax.all_gather(masked, "rep", axis=1, tiled=True)
    width = levels * B
    stacked = gathered.reshape(width, points)
    square = [(B, B), (B, B)]
    lower, inverse, logs = call(
        factor_kernel, "leaf_factor", [(points, points), (points, B), (T, B)], square, leaf_blocks
    )
    half, reduced = call(
        leaf_kernel,
        "leaf_reduce",
        [(width + count, points), (width + count + T, width)],
        [],
        stacked,
        rhs,
        order,
        lower,
        inverse,
        logs,
    )
    invs, ys = [], []
    for depth in range(levels):
        received = swapped(reduced, "leaf", depth)
        left = (levels - depth - 1) * B
        following = (left + count + T, left) if left else (T, B)
        pivot_inverse, pivot_right, reduced = call(
            functools.partial(level_kernel, depth, count),
            "level_%d" % depth,
            [(B, B), (left + count, B), following],
            square,
            reduced,
            received,
        )
        invs.append(pivot_inverse)
        ys.append(pivot_right)
    leaf_count = lax.axis_size("leaf")
    terms = [leaf_count * points] + [leaf_count // 2 ** (depth + 1) * B for depth in range(levels)]
    determinants = reduced[0, : levels + 1] / jnp.array(terms, jnp.float32)
    (solution,) = call(
        functools.partial(back_kernel, levels),
        "back_solve",
        [(count, points)],
        [(count, width), (count, points)],
        *invs,
        *ys,
        half,
        lower,
        inverse,
        order,
    )
    return (solution, determinants)


def solution(mesh):
    placed = (
        P("leaf", None),
        P(None, "rep", "leaf"),
        P("rep", "leaf"),
        P("leaf", None),
        P(None, "leaf"),
    )
    return jax.shard_map(
        shards, mesh=mesh, in_specs=placed, out_specs=(P("rep", "leaf"), P()), check_vma=False
    )
```

```python
import functools

import jax
import jax.numpy as jnp
from jax import lax
from jax.experimental import pallas as pl
from jax.experimental.pallas import tpu as pltpu
from jax.sharding import PartitionSpec as P

HIGHEST = lax.Precision.HIGHEST
B = 128
T = 8


def swapped(value, axis, bit):
    mask = 2**bit
    pairs = [(source, source ^ mask) for source in range(lax.axis_size(axis))]
    return lax.ppermute(value, axis, pairs)


def dot_nn(left, right):
    return jnp.dot(left, right, precision=HIGHEST, preferred_element_type=jnp.float32)


def dot_nt(left, right):
    return lax.dot_general(
        left, right, (((1,), (1,)), ((), ())), precision=HIGHEST, preferred_element_type=jnp.float32
    )


def spread(row):
    return jnp.broadcast_to(row, (T, B))


def eliminate(s_ref, t_ref):
    sub = lax.broadcasted_iota(jnp.int32, (T, B), 0)
    rows = lax.broadcasted_iota(jnp.int32, (B, B), 0)
    lanes = lax.broadcasted_iota(jnp.int32, (B, B), 1)
    t_ref[...] = jnp.where(rows == lanes, 1.0, 0.0).astype(jnp.float32)
    logs = jnp.zeros((T, B), jnp.float32)
    for tile in range(B // T):
        lo = tile * T
        p = s_ref[lo : lo + T, :]
        q = t_ref[lo : lo + T, :]
        cols = [spread(p[:, lo + j : lo + j + 1]) for j in range(T)]
        diag = jnp.zeros((T, B), jnp.float32)
        for j in range(T):
            pivot = spread(cols[j][j : j + 1])
            diag = jnp.where(sub == j, pivot, diag)
            if j < T - 1:
                factor = jnp.where(sub > j, cols[j] * (1.0 / pivot), 0.0)
                for other in range(j + 1, T):
                    cols[other] = cols[other] - factor * spread(cols[other][j : j + 1])
                p = p - factor * spread(p[j : j + 1])
                q = q - factor * spread(q[j : j + 1])
        logs = logs + jnp.log(diag)
        t_ref[lo : lo + T, :] = q * lax.rsqrt(diag)
        if lo + T < B:
            inverse = 1.0 / diag
            p = p * inverse
            q = q * inverse
            for j in range(T - 1, 0, -1):
                factor = jnp.where(sub < j, cols[j] * inverse, 0.0)
                p = p - factor * spread(p[j : j + 1])
                q = q - factor * spread(q[j : j + 1])
            p_rows = [spread(p[j : j + 1]) for j in range(T)]
            q_rows = [spread(q[j : j + 1]) for j in range(T)]
            for below in range(tile + 1, B // T):
                at = below * T
                s_tile = s_ref[at : at + T, :]
                t_tile = t_ref[at : at + T, :]
                s_sum = jnp.zeros((T, B), jnp.float32)
                t_sum = jnp.zeros((T, B), jnp.float32)
                for j in range(T):
                    column = spread(s_tile[:, lo + j : lo + j + 1])
                    s_sum = s_sum + column * p_rows[j]
                    t_sum = t_sum + column * q_rows[j]
                s_ref[at : at + T, :] = s_tile - s_sum
                t_ref[at : at + T, :] = t_tile - t_sum
    return logs


def split(value):
    high = value.astype(jnp.bfloat16)
    return high, (value - high.astype(jnp.float32)).astype(jnp.bfloat16)


def pieces(value):
    high, _ = split(value)
    rest = value - high.astype(jnp.float32)
    middle, low = split(rest)
    return jnp.concatenate([high, middle, low], axis=0)


def one_nt(left, right):
    return lax.dot_general(
        left, right, (((1,), (1,)), ((), ())), preferred_element_type=jnp.float32
    )


def one_nn(left, right):
    return jnp.dot(left, right, preferred_element_type=jnp.float32)


def three(one, left, right):
    return one(left[0], right[0]) + (one(left[0], right[1]) + one(left[1], right[0]))


def columns(blocks, count):
    starts = [0]
    for j in range(blocks):
        starts.append(starts[-1] + (blocks - j) * B + count)
    return starts


def factor_kernel(d_ref, hi_ref, lo_ref, inv_ref, log_ref, l_ref, s_ref, t_ref):
    points = d_ref.shape[0]
    blocks = points // B
    l_ref[...] = d_ref[...]

    def panel(j, logs):
        at = pl.multiple_of(j * B, B)
        s_ref[...] = l_ref[pl.ds(at, B), pl.ds(at, B)]
        logs = logs + eliminate(s_ref, t_ref)
        inv_ref[pl.ds(at, B), :] = t_ref[...]
        for own in range(blocks - 1):
            lo = (own + 1) * B
            here = slice(own * B, lo)

            @pl.when(j == own)
            def _():
                inverse = split(t_ref[...])

                @pl.loop(own + 1, blocks)
                def _(r):
                    rows = pl.ds(pl.multiple_of(r * B, B), B)
                    high, low = split(three(one_nt, split(l_ref[rows, here]), inverse))
                    hi_ref[rows, here] = high
                    lo_ref[rows, here] = low

                for first in range(lo, points, 2 * B):
                    last = min(first + 2 * B, points)

                    @pl.loop(first // B, blocks)
                    def _(r):
                        rows = pl.ds(pl.multiple_of(r * B, B), B)
                        l_ref[rows, first:last] = l_ref[rows, first:last] - three(
                            one_nt,
                            (hi_ref[rows, here], lo_ref[rows, here]),
                            (hi_ref[first:last, here], lo_ref[first:last, here]),
                        )

        return logs

    logs = lax.fori_loop(0, blocks, panel, jnp.zeros((T, B), jnp.float32))
    log_ref[...] = jnp.broadcast_to(jnp.sum(logs, axis=0, keepdims=True), (T, B))


def leaf_kernel(
    a_ref, r_ref, order_ref, hi_ref, lo_ref, inv_ref, log_ref, xh_ref, xl_ref, xr_ref, red_ref, x_ref
):
    width, points = a_ref.shape
    count = r_ref.shape[0]
    total = width + count
    sensor = lax.broadcasted_iota(jnp.int32, (points, B), 0)
    cut = pieces(r_ref[...])
    for lo in range(0, points, B):
        pick = jnp.where(sensor == order_ref[0:1, lo : lo + B], 1.0, 0.0).astype(jnp.bfloat16)
        part = one_nn(cut, pick)
        x_ref[width:, lo : lo + B] = (
            part[:count] + part[count : 2 * count] + part[2 * count :]
        )
        x_ref[:width, lo : lo + B] = a_ref[:, lo : lo + B]
    step = total // 5
    for lo in range(0, points, 2 * B):
        middle, hi = lo + B, lo + 2 * B
        first = split(inv_ref[lo:middle, :])
        second = split(inv_ref[middle:hi, :])

        @pl.loop(0, 5)
        def _(r):
            rows = pl.ds(pl.multiple_of(r * step, 2 * T), step)
            value = x_ref[rows, lo:hi]
            if lo > 0:
                value = value - three(
                    one_nt,
                    (xh_ref[rows, :lo], xl_ref[rows, :lo]),
                    (hi_ref[lo:hi, :lo], lo_ref[lo:hi, :lo]),
                )
            solved = three(one_nt, split(value[:, :B]), first)
            x_ref[rows, lo:middle] = solved
            high, low = split(solved)
            xh_ref[rows, lo:middle] = high
            xl_ref[rows, lo:middle] = low
            rest = value[:, B:] - three(
                one_nt, (high, low), (hi_ref[middle:hi, lo:middle], lo_ref[middle:hi, lo:middle])
            )
            solved = three(one_nt, split(rest), second)
            x_ref[rows, middle:hi] = solved
            high, low = split(solved)
            xh_ref[rows, middle:hi] = high
            xl_ref[rows, middle:hi] = low

    xr_ref[...] = x_ref[width:, :]
    starts = columns(width // B, count)
    for j in range(0, width // B, 2):
        lo, middle, hi = j * B, (j + 1) * B, (j + 2) * B
        right = (xh_ref[lo:hi, :], xl_ref[lo:hi, :])

        def put(rows, at, size, both):
            value = three(one_nt, (xh_ref[rows, :], xl_ref[rows, :]), right)
            red_ref[pl.ds(starts[j] + at, size), :] = value[:, :B]
            if both:
                red_ref[pl.ds(starts[j + 1] + at - B, size), :] = value[:, B:]

        put(slice(lo, middle), 0, B, False)

        @pl.loop(j + 1, width // B)
        def _(r):
            put(pl.ds(pl.multiple_of(r * B, B), B), pl.multiple_of((r - j) * B, B), B, True)

        put(slice(width, total), width - lo, count, True)
    lane = lax.broadcasted_iota(jnp.int32, (T, B), 1)
    red_ref[starts[-1] :, :] = jnp.where(lane == 0, log_ref[...], 0.0)


def level_kernel(depth, levels, count, own_ref, other_ref, inv_ref, y_ref, out_ref, s_ref, t_ref):
    blocks = levels - depth
    left = (blocks - 1) * B
    starts = columns(blocks, count)
    after = columns(blocks - 1, count)
    rows = lax.broadcasted_iota(jnp.int32, (B, B), 0)
    lanes = lax.broadcasted_iota(jnp.int32, (B, B), 1)
    eye = jnp.where(rows == lanes, 1.0, 0.0).astype(jnp.float32)
    s_ref[...] = eye + (own_ref[:B, :] + other_ref[:B, :])
    logs = eliminate(s_ref, t_ref)
    inv_ref[...] = t_ref[...]
    end = starts[1]
    y_ref[...] = dot_nt(own_ref[B:end, :] + other_ref[B:end, :], t_ref[...])
    sums = own_ref[starts[-1] :, :] + other_ref[starts[-1] :, :]
    lane = lax.broadcasted_iota(jnp.int32, (T, B), 1)
    total = jnp.sum(logs, axis=0, keepdims=True)
    out_ref[after[-1] :, :] = jnp.where(lane == depth + 1, total, sums)
    for j in range(blocks - 1):
        source = slice(starts[j + 1], starts[j + 2])
        out_ref[after[j] : after[j + 1], :] = (own_ref[source, :] + other_ref[source, :]) - dot_nt(
            y_ref[j * B :, :], y_ref[j * B : (j + 1) * B, :]
        )


def back_kernel(levels, *refs):
    invs = refs[:levels]
    ys = refs[levels : 2 * levels]
    xh_ref, xl_ref, xr_ref, hi_ref, lo_ref, inv_ref, order_ref, out_ref, c_ref, z_ref = refs[
        2 * levels :
    ]
    count, points = out_ref.shape
    width = levels * B
    for depth in reversed(range(levels)):
        left = (levels - depth - 1) * B
        target = ys[depth][left:, :]
        lo = depth * B
        if left > 0:
            target = target - dot_nn(c_ref[:, lo + B :], ys[depth][:left, :])
        c_ref[:, lo : lo + B] = dot_nn(target, invs[depth][...])
    coefficients = split(c_ref[...])
    for lo in range(0, points, 2 * B):
        here = slice(lo, lo + 2 * B)
        z_ref[:, here] = xr_ref[:, here] - three(
            one_nn, coefficients, (xh_ref[:width, here], xl_ref[:width, here])
        )
    for lo in reversed(range(0, points, B)):
        hi = lo + B
        value = z_ref[:, lo:hi]
        if hi < points:
            value = value - three(
                one_nn, split(z_ref[:, hi:]), (hi_ref[hi:, lo:hi], lo_ref[hi:, lo:hi])
            )
        z_ref[:, lo:hi] = dot_nn(value, inv_ref[lo:hi, :])
    sensor = lax.broadcasted_iota(jnp.int32, (points, 2 * B), 0)
    for lo in range(0, points, 2 * B):
        hi = lo + 2 * B
        pick = jnp.where(sensor == order_ref[0:1, lo:hi], 1.0, 0.0).astype(jnp.bfloat16)
        part = one_nt(pieces(z_ref[:, lo:hi]), pick)
        part = part[:count] + part[count : 2 * count] + part[2 * count :]
        out_ref[...] = part if lo == 0 else out_ref[...] + part


def call(kernel, name, outs, scratch, *operands):
    typed = [out if isinstance(out[0], tuple) else (out, jnp.float32) for out in outs]
    return pl.pallas_call(
        kernel,
        name=name,
        out_shape=[jax.ShapeDtypeStruct(*out) for out in typed],
        in_specs=[pl.BlockSpec(memory_space=pltpu.VMEM)] * len(operands),
        out_specs=[pl.BlockSpec(memory_space=pltpu.VMEM)] * len(outs),
        scratch_shapes=[pltpu.VMEM(shape, jnp.float32) for shape in scratch],
        compiler_params=pltpu.CompilerParams(vmem_limit_bytes=48 * 2**20),
    )(*operands)


def shards(leaf_blocks, generators, rhs, order, ranks):
    levels, quarter, points = generators.shape
    count = rhs.shape[0]
    replica = lax.axis_index("rep")
    rank_index = lax.broadcasted_iota(jnp.int32, (levels, quarter, 1), 1) + replica * quarter
    masked = jnp.where(rank_index < ranks[:, :, None], generators, 0.0)
    gathered = lax.all_gather(masked, "rep", axis=1, tiled=True)
    width = levels * B
    stacked = gathered.reshape(width, points)
    square = [(B, B), (B, B)]
    narrow = ((points, points), jnp.bfloat16)
    high, low, inverse, logs = call(
        factor_kernel,
        "leaf_factor",
        [narrow, narrow, (points, B), (T, B)],
        [(points, points)] + square,
        leaf_blocks,
    )
    narrow = ((width + count, points), jnp.bfloat16)
    half_high, half_low, half_right, reduced = call(
        leaf_kernel,
        "leaf_reduce",
        [narrow, narrow, (count, points), (columns(levels, count)[-1] + T, B)],
        [(width + count, points)],
        stacked,
        rhs,
        order,
        high,
        low,
        inverse,
        logs,
    )
    invs, ys = [], []
    for depth in range(levels):
        received = swapped(reduced, "leaf", depth)
        left = (levels - depth - 1) * B
        pivot_inverse, pivot_right, reduced = call(
            functools.partial(level_kernel, depth, levels, count),
            "level_%d" % depth,
            [(B, B), (left + count, B), (columns(levels - depth - 1, count)[-1] + T, B)],
            square,
            reduced,
            received,
        )
        invs.append(pivot_inverse)
        ys.append(pivot_right)
    leaf_count = lax.axis_size("leaf")
    terms = [leaf_count * points] + [leaf_count // 2 ** (depth + 1) * B for depth in range(levels)]
    determinants = reduced[0, : levels + 1] / jnp.array(terms, jnp.float32)
    (solution,) = call(
        functools.partial(back_kernel, levels),
        "back_solve",
        [(count, points)],
        [(count, width), (count, points)],
        *invs,
        *ys,
        half_high,
        half_low,
        half_right,
        high,
        low,
        inverse,
        order,
    )
    return (solution, determinants)


def solution(mesh):
    placed = (
        P("leaf", None),
        P(None, "rep", "leaf"),
        P("rep", "leaf"),
        P("leaf", None),
        P(None, "leaf"),
    )
    return jax.shard_map(
        shards, mesh=mesh, in_specs=placed, out_specs=(P("rep", "leaf"), P()), check_vma=False
    )
```

```python
import functools

import jax
import jax.numpy as jnp
from jax import lax
from jax.experimental import pallas as pl
from jax.experimental.pallas import tpu as pltpu
from jax.sharding import PartitionSpec as P

HIGHEST = lax.Precision.HIGHEST
B = 128
T = 8
TAIL = 16
HALVED = (1, 2)


def swapped(value, axis, bit):
    mask = 2**bit
    pairs = [(source, source ^ mask) for source in range(lax.axis_size(axis))]
    return lax.ppermute(value, axis, pairs)


def dot_nn(left, right):
    return jnp.dot(left, right, precision=HIGHEST, preferred_element_type=jnp.float32)


def dot_nt(left, right):
    return lax.dot_general(
        left, right, (((1,), (1,)), ((), ())), precision=HIGHEST, preferred_element_type=jnp.float32
    )


def spread(row):
    return jnp.broadcast_to(row, (T, B))


def eliminate(s_ref, t_ref):
    sub = lax.broadcasted_iota(jnp.int32, (T, B), 0)
    rows = lax.broadcasted_iota(jnp.int32, (B, B), 0)
    lanes = lax.broadcasted_iota(jnp.int32, (B, B), 1)
    t_ref[...] = jnp.where(rows == lanes, 1.0, 0.0).astype(jnp.float32)
    logs = jnp.zeros((T, B), jnp.float32)
    for tile in range(B // T):
        lo = tile * T
        p = s_ref[lo : lo + T, :]
        q = t_ref[lo : lo + T, :]
        cols = [spread(p[:, lo + j : lo + j + 1]) for j in range(T)]
        diag = jnp.zeros((T, B), jnp.float32)
        for j in range(T):
            pivot = spread(cols[j][j : j + 1])
            diag = jnp.where(sub == j, pivot, diag)
            if j < T - 1:
                factor = jnp.where(sub > j, cols[j] * (1.0 / pivot), 0.0)
                for other in range(j + 1, T):
                    cols[other] = cols[other] - factor * spread(cols[other][j : j + 1])
                p = p - factor * spread(p[j : j + 1])
                q = q - factor * spread(q[j : j + 1])
        logs = logs + jnp.log(diag)
        t_ref[lo : lo + T, :] = q * lax.rsqrt(diag)
        if lo + T < B:
            inverse = 1.0 / diag
            p = p * inverse
            q = q * inverse
            for j in range(T - 1, 0, -1):
                factor = jnp.where(sub < j, cols[j] * inverse, 0.0)
                p = p - factor * spread(p[j : j + 1])
                q = q - factor * spread(q[j : j + 1])
            p_rows = [spread(p[j : j + 1]) for j in range(T)]
            q_rows = [spread(q[j : j + 1]) for j in range(T)]
            for below in range(tile + 1, B // T):
                at = below * T
                s_tile = s_ref[at : at + T, :]
                t_tile = t_ref[at : at + T, :]
                s_sum = jnp.zeros((T, B), jnp.float32)
                t_sum = jnp.zeros((T, B), jnp.float32)
                for j in range(T):
                    column = spread(s_tile[:, lo + j : lo + j + 1])
                    s_sum = s_sum + column * p_rows[j]
                    t_sum = t_sum + column * q_rows[j]
                s_ref[at : at + T, :] = s_tile - s_sum
                t_ref[at : at + T, :] = t_tile - t_sum
    return logs


def split(value):
    high = value.astype(jnp.bfloat16)
    return high, (value - high.astype(jnp.float32)).astype(jnp.bfloat16)


def pieces(value):
    high, _ = split(value)
    rest = value - high.astype(jnp.float32)
    middle, low = split(rest)
    return jnp.concatenate([high, middle, low], axis=0)


def one_nt(left, right):
    return lax.dot_general(
        left, right, (((1,), (1,)), ((), ())), preferred_element_type=jnp.float32
    )


def one_nn(left, right):
    return jnp.dot(left, right, preferred_element_type=jnp.float32)


def three(one, left, right):
    return one(left[0], right[0]) + (one(left[0], right[1]) + one(left[1], right[0]))


def columns(blocks, count):
    starts = [-B]
    for j in range(blocks):
        starts.append(starts[-1] + (blocks - j) * B + count)
    return starts if blocks else [0]


def packed(blocks, count):
    return columns(blocks, count)[-1] + TAIL


def factor_kernel(d_ref, hi_ref, lo_ref, inv_ref, log_ref, l_ref, s_ref, t_ref):
    points = d_ref.shape[0]
    blocks = points // B
    l_ref[...] = d_ref[...]

    def panel(j, logs):
        at = pl.multiple_of(j * B, B)
        s_ref[...] = l_ref[pl.ds(at, B), pl.ds(at, B)]
        logs = logs + eliminate(s_ref, t_ref)
        inv_ref[pl.ds(at, B), :] = t_ref[...]
        for own in range(blocks - 1):
            lo = (own + 1) * B
            here = slice(own * B, lo)

            @pl.when(j == own)
            def _():
                inverse = split(t_ref[...])

                @pl.loop(own + 1, blocks)
                def _(r):
                    rows = pl.ds(pl.multiple_of(r * B, B), B)
                    high, low = split(three(one_nt, split(l_ref[rows, here]), inverse))
                    hi_ref[rows, here] = high
                    lo_ref[rows, here] = low

                for first in range(lo, points, 2 * B):
                    last = min(first + 2 * B, points)

                    @pl.loop(first // B, blocks)
                    def _(r):
                        rows = pl.ds(pl.multiple_of(r * B, B), B)
                        l_ref[rows, first:last] = l_ref[rows, first:last] - three(
                            one_nt,
                            (hi_ref[rows, here], lo_ref[rows, here]),
                            (hi_ref[first:last, here], lo_ref[first:last, here]),
                        )

        return logs

    logs = lax.fori_loop(0, blocks, panel, jnp.zeros((T, B), jnp.float32))
    log_ref[...] = jnp.broadcast_to(jnp.sum(logs, axis=0, keepdims=True), (T, B))


def leaf_kernel(
    a_ref, r_ref, order_ref, hi_ref, lo_ref, inv_ref, log_ref, xh_ref, xl_ref, xr_ref, diag_ref, red_ref, x_ref
):
    width, points = a_ref.shape
    count = r_ref.shape[0]
    total = width + count
    sensor = lax.broadcasted_iota(jnp.int32, (points, B), 0)
    cut = pieces(r_ref[...])
    for lo in range(0, points, B):
        pick = jnp.where(sensor == order_ref[0:1, lo : lo + B], 1.0, 0.0).astype(jnp.bfloat16)
        part = one_nn(cut, pick)
        x_ref[width:, lo : lo + B] = (
            part[:count] + part[count : 2 * count] + part[2 * count :]
        )
        x_ref[:width, lo : lo + B] = a_ref[:, lo : lo + B]
    step = total // 5
    for lo in range(0, points, 2 * B):
        middle, hi = lo + B, lo + 2 * B
        first = split(inv_ref[lo:middle, :])
        second = split(inv_ref[middle:hi, :])

        @pl.loop(0, 5)
        def _(r):
            rows = pl.ds(pl.multiple_of(r * step, 2 * T), step)
            value = x_ref[rows, lo:hi]
            if lo > 0:
                value = value - three(
                    one_nt,
                    (xh_ref[rows, :lo], xl_ref[rows, :lo]),
                    (hi_ref[lo:hi, :lo], lo_ref[lo:hi, :lo]),
                )
            solved = three(one_nt, split(value[:, :B]), first)
            x_ref[rows, lo:middle] = solved
            high, low = split(solved)
            xh_ref[rows, lo:middle] = high
            xl_ref[rows, lo:middle] = low
            rest = value[:, B:] - three(
                one_nt, (high, low), (hi_ref[middle:hi, lo:middle], lo_ref[middle:hi, lo:middle])
            )
            solved = three(one_nt, split(rest), second)
            x_ref[rows, middle:hi] = solved
            high, low = split(solved)
            xh_ref[rows, middle:hi] = high
            xl_ref[rows, middle:hi] = low

    xr_ref[...] = x_ref[width:, :]
    starts = columns(width // B, count)
    for j in range(0, width // B, 2):
        lo, middle, hi = j * B, (j + 1) * B, (j + 2) * B
        right = (xh_ref[lo:hi, :], xl_ref[lo:hi, :])

        def put(rows, at, size, both):
            value = three(one_nt, (xh_ref[rows, :], xl_ref[rows, :]), right)
            if j == 0 and not both:
                diag_ref[...] = value[:, :B]
            else:
                red_ref[pl.ds(starts[j] + at, size), :] = value[:, :B]
            if both:
                red_ref[pl.ds(starts[j + 1] + at - B, size), :] = value[:, B:]

        put(slice(lo, middle), 0, B, False)

        @pl.loop(j + 1, width // B)
        def _(r):
            put(pl.ds(pl.multiple_of(r * B, B), B), pl.multiple_of((r - j) * B, B), B, True)

        put(slice(width, total), width - lo, count, True)
    lane = lax.broadcasted_iota(jnp.int32, (TAIL, B), 1)
    red_ref[starts[-1] :, :] = jnp.where(lane == 0, log_ref[0:1, :], 0.0)


def pivot_kernel(own_ref, other_ref, inv_ref, log_ref, s_ref):
    rows = lax.broadcasted_iota(jnp.int32, (B, B), 0)
    lanes = lax.broadcasted_iota(jnp.int32, (B, B), 1)
    eye = jnp.where(rows == lanes, 1.0, 0.0).astype(jnp.float32)
    s_ref[...] = eye + (own_ref[...] + other_ref[...])
    logs = eliminate(s_ref, inv_ref)
    log_ref[...] = jnp.broadcast_to(jnp.sum(logs, axis=0, keepdims=True), (T, B))


def head_kernel(blocks, count, halved, core_ref, own_ref, *refs):
    others, refs = refs[: 2 if halved else 1], refs[2 if halved else 1 :]
    inv_ref, y_ref, diag_ref, sum_ref = refs
    starts = columns(blocks, count)
    if halved:
        first = core_ref[0, 0] == 0
        half = own_ref.shape[0] // 2
        near, far = others[0][...], others[1][...]
        sum_ref[:half, :] = own_ref[:half, :] + jnp.where(first, near, far)
        sum_ref[half:, :] = own_ref[half:, :] + jnp.where(first, far, near)
    else:
        sum_ref[...] = own_ref[...] + others[0][...]
    y_ref[...] = dot_nt(sum_ref[: starts[1], :], inv_ref[...])
    if blocks > 1:
        at = starts[1]
        diag_ref[...] = sum_ref[at : at + B, :] - dot_nt(y_ref[:B, :], y_ref[:B, :])
    else:
        diag_ref[...] = jnp.zeros((B, B), jnp.float32)


def rest_kernel(depth, blocks, count, core_ref, sum_ref, y_ref, log_ref, out_ref, *half_refs):
    starts = columns(blocks, count)
    after = columns(blocks - 1, count)
    lane = lax.broadcasted_iota(jnp.int32, (TAIL, B), 1)
    out_ref[after[-1] :, :] = jnp.where(
        lane == depth + 1, log_ref[0:1, :], sum_ref[starts[-1] :, :]
    )
    for j in range(blocks - 1):
        skip = B if j == 0 else 0
        out_ref[after[j] + skip : after[j + 1], :] = sum_ref[
            starts[j + 1] + skip : starts[j + 2], :
        ] - dot_nt(y_ref[j * B + skip :, :], y_ref[j * B : (j + 1) * B, :])
    if half_refs:
        half = half_refs[0].shape[0]
        first = core_ref[0, 0] == 0
        half_refs[0][...] = jnp.where(first, out_ref[:half, :], out_ref[half:, :])


def back_kernel(levels, *refs):
    invs = refs[:levels]
    ys = refs[levels : 2 * levels]
    xh_ref, xl_ref, xr_ref, hi_ref, lo_ref, inv_ref, order_ref, out_ref, c_ref, z_ref = refs[
        2 * levels :
    ]
    count, points = out_ref.shape
    width = levels * B
    for depth in reversed(range(levels)):
        left = (levels - depth - 1) * B
        target = ys[depth][left:, :]
        lo = depth * B
        if left > 0:
            target = target - dot_nn(c_ref[:, lo + B :], ys[depth][:left, :])
        c_ref[:, lo : lo + B] = dot_nn(target, invs[depth][...])
    coefficients = split(c_ref[...])
    for lo in range(0, points, 2 * B):
        here = slice(lo, lo + 2 * B)
        z_ref[:, here] = xr_ref[:, here] - three(
            one_nn, coefficients, (xh_ref[:width, here], xl_ref[:width, here])
        )
    for lo in reversed(range(0, points, B)):
        hi = lo + B
        value = z_ref[:, lo:hi]
        if hi < points:
            value = value - three(
                one_nn, split(z_ref[:, hi:]), (hi_ref[hi:, lo:hi], lo_ref[hi:, lo:hi])
            )
        z_ref[:, lo:hi] = dot_nn(value, inv_ref[lo:hi, :])
    sensor = lax.broadcasted_iota(jnp.int32, (points, 2 * B), 0)
    for lo in range(0, points, 2 * B):
        hi = lo + 2 * B
        pick = jnp.where(sensor == order_ref[0:1, lo:hi], 1.0, 0.0).astype(jnp.bfloat16)
        part = one_nt(pieces(z_ref[:, lo:hi]), pick)
        part = part[:count] + part[count : 2 * count] + part[2 * count :]
        out_ref[...] = part if lo == 0 else out_ref[...] + part


def call(kernel, name, outs, scratch, *operands, smem=0, work=None, limit=48):
    typed = [out if isinstance(out[0], tuple) else (out, jnp.float32) for out in outs]
    return pl.pallas_call(
        kernel,
        name=name,
        out_shape=[jax.ShapeDtypeStruct(*out) for out in typed],
        in_specs=[pl.BlockSpec(memory_space=pltpu.SMEM)] * smem
        + [pl.BlockSpec(memory_space=pltpu.VMEM)] * (len(operands) - smem),
        out_specs=[pl.BlockSpec(memory_space=pltpu.VMEM)] * len(outs),
        scratch_shapes=[pltpu.VMEM(shape, jnp.float32) for shape in scratch],
        compiler_params=pltpu.CompilerParams(vmem_limit_bytes=limit * 2**20),
        cost_estimate=work,
    )(*operands)


def shards(leaf_blocks, generators, rhs, order, ranks):
    levels, quarter, points = generators.shape
    count = rhs.shape[0]
    replica = lax.axis_index("rep")
    rank_index = lax.broadcasted_iota(jnp.int32, (levels, quarter, 1), 1) + replica * quarter
    masked = jnp.where(rank_index < ranks[:, :, None], generators, 0.0)
    gathered = lax.all_gather(masked, "rep", axis=1, tiled=True)
    width = levels * B
    stacked = gathered.reshape(width, points)
    square = [(B, B), (B, B)]
    narrow = ((points, points), jnp.bfloat16)
    high, low, inverse, logs = call(
        factor_kernel,
        "leaf_factor",
        [narrow, narrow, (points, B), (T, B)],
        [(points, points)] + square,
        leaf_blocks,
    )
    narrow = ((width + count, points), jnp.bfloat16)
    half_high, half_low, half_right, diagonal, reduced = call(
        leaf_kernel,
        "leaf_reduce",
        [narrow, narrow, (count, points), (B, B), (packed(levels, count), B)],
        [(width + count, points)],
        stacked,
        rhs,
        order,
        high,
        low,
        inverse,
        logs,
    )
    invs, ys = [], []
    core = (lax.axis_index("leaf") % 2).astype(jnp.int32).reshape(1, 1)
    work = pl.CostEstimate(flops=2**22, bytes_accessed=2**24, transcendentals=0)
    short = pl.CostEstimate(flops=2**22, bytes_accessed=2**22, transcendentals=0)
    part = None
    for depth in range(levels):
        blocks = levels - depth
        left = (blocks - 1) * B
        halved = depth in HALVED
        other = swapped(diagonal, "leaf", depth)
        sent = part if halved else reduced
        if depth < levels - 1:
            sent, other = lax.optimization_barrier((sent, other))
        near = swapped(sent, "leaf", depth)
        pivot_inverse, logs = call(
            pivot_kernel, "pivot", [(B, B), (T, B)], [(B, B)], diagonal, other, work=work, limit=12
        )
        received = [near]
        if halved:
            near, pivot_inverse = lax.optimization_barrier((near, pivot_inverse))
            received = [near, swapped(near, "leaf", 0)]
        pivot_right, diagonal, sums = call(
            functools.partial(head_kernel, blocks, count, halved),
            "head_%d" % depth,
            [(left + count, B), (B, B), (packed(blocks, count), B)],
            [],
            core,
            reduced,
            *received,
            pivot_inverse,
            smem=1,
            work=short,
            limit=12,
        )
        following = packed(blocks - 1, count)
        halving = depth + 1 in HALVED and depth + 1 < levels
        reduced, *parts = call(
            functools.partial(rest_kernel, depth, blocks, count),
            "rest_%d" % depth,
            [(following, B)] + [(following // 2, B)] * halving,
            [],
            core,
            sums,
            pivot_right,
            logs,
            smem=1,
            work=short,
            limit=12,
        )
        part = parts[0] if halving else None
        invs.append(pivot_inverse)
        ys.append(pivot_right)
    leaf_count = lax.axis_size("leaf")
    terms = [leaf_count * points] + [leaf_count // 2 ** (depth + 1) * B for depth in range(levels)]
    determinants = reduced[0, : levels + 1] / jnp.array(terms, jnp.float32)
    (solution,) = call(
        functools.partial(back_kernel, levels),
        "back_solve",
        [(count, points)],
        [(count, width), (count, points)],
        *invs,
        *ys,
        half_high,
        half_low,
        half_right,
        high,
        low,
        inverse,
        order,
        limit=24,
    )
    return (solution, determinants)


def solution(mesh):
    placed = (
        P("leaf", None),
        P(None, "rep", "leaf"),
        P("rep", "leaf"),
        P("leaf", None),
        P(None, "leaf"),
    )
    return jax.shard_map(
        shards, mesh=mesh, in_specs=placed, out_specs=(P("rep", "leaf"), P()), check_vma=False
    )
```

```python
import functools

import jax
import jax.numpy as jnp
from jax import lax
from jax.experimental import pallas as pl
from jax.experimental.pallas import tpu as pltpu
from jax.sharding import PartitionSpec as P

HIGHEST = lax.Precision.HIGHEST
B = 128
T = 8
TAIL = 16
HALVED = (1, 2)


def swapped(value, axis, bit):
    mask = 2**bit
    pairs = [(source, source ^ mask) for source in range(lax.axis_size(axis))]
    return lax.ppermute(value, axis, pairs)


def dot_nn(left, right):
    return jnp.dot(left, right, precision=HIGHEST, preferred_element_type=jnp.float32)


def dot_nt(left, right):
    return lax.dot_general(
        left, right, (((1,), (1,)), ((), ())), precision=HIGHEST, preferred_element_type=jnp.float32
    )


def spread(row):
    return jnp.broadcast_to(row, (T, B))


def eliminate(s_ref, t_ref):
    sub = lax.broadcasted_iota(jnp.int32, (T, B), 0)
    rows = lax.broadcasted_iota(jnp.int32, (B, B), 0)
    lanes = lax.broadcasted_iota(jnp.int32, (B, B), 1)
    t_ref[...] = jnp.where(rows == lanes, 1.0, 0.0).astype(jnp.float32)
    logs = jnp.zeros((T, B), jnp.float32)
    for tile in range(B // T):
        lo = tile * T
        p = s_ref[lo : lo + T, :]
        q = t_ref[lo : lo + T, :]
        cols = [spread(p[:, lo + j : lo + j + 1]) for j in range(T)]
        diag = jnp.zeros((T, B), jnp.float32)
        for j in range(T):
            pivot = spread(cols[j][j : j + 1])
            diag = jnp.where(sub == j, pivot, diag)
            if j < T - 1:
                factor = jnp.where(sub > j, cols[j] * (1.0 / pivot), 0.0)
                for other in range(j + 1, T):
                    cols[other] = cols[other] - factor * spread(cols[other][j : j + 1])
                p = p - factor * spread(p[j : j + 1])
                q = q - factor * spread(q[j : j + 1])
        logs = logs + jnp.log(diag)
        t_ref[lo : lo + T, :] = q * lax.rsqrt(diag)
        if lo + T < B:
            inverse = 1.0 / diag
            p = p * inverse
            q = q * inverse
            for j in range(T - 1, 0, -1):
                factor = jnp.where(sub < j, cols[j] * inverse, 0.0)
                p = p - factor * spread(p[j : j + 1])
                q = q - factor * spread(q[j : j + 1])
            p_rows = [spread(p[j : j + 1]) for j in range(T)]
            q_rows = [spread(q[j : j + 1]) for j in range(T)]
            for below in range(tile + 1, B // T):
                at = below * T
                s_tile = s_ref[at : at + T, :]
                t_tile = t_ref[at : at + T, :]
                s_sum = jnp.zeros((T, B), jnp.float32)
                t_sum = jnp.zeros((T, B), jnp.float32)
                for j in range(T):
                    column = spread(s_tile[:, lo + j : lo + j + 1])
                    s_sum = s_sum + column * p_rows[j]
                    t_sum = t_sum + column * q_rows[j]
                s_ref[at : at + T, :] = s_tile - s_sum
                t_ref[at : at + T, :] = t_tile - t_sum
    return logs


def split(value):
    high = value.astype(jnp.bfloat16)
    return high, (value - high.astype(jnp.float32)).astype(jnp.bfloat16)


def pieces(value):
    high, _ = split(value)
    rest = value - high.astype(jnp.float32)
    middle, low = split(rest)
    return jnp.concatenate([high, middle, low], axis=0)


def one_nt(left, right):
    return lax.dot_general(
        left, right, (((1,), (1,)), ((), ())), preferred_element_type=jnp.float32
    )


def one_nn(left, right):
    return jnp.dot(left, right, preferred_element_type=jnp.float32)


def three(one, left, right):
    return one(left[0], right[0]) + (one(left[0], right[1]) + one(left[1], right[0]))


def columns(blocks, count):
    starts = [-B]
    for j in range(blocks):
        starts.append(starts[-1] + (blocks - j) * B + count)
    return starts if blocks else [0]


def packed(blocks, count):
    return columns(blocks, count)[-1] + TAIL


def factor_kernel(d_ref, hi_ref, lo_ref, inv_ref, log_ref, l_ref, s_ref, t_ref):
    points = d_ref.shape[0]
    blocks = points // B
    l_ref[...] = d_ref[...]

    def panel(j, logs):
        at = pl.multiple_of(j * B, B)
        s_ref[...] = l_ref[pl.ds(at, B), pl.ds(at, B)]
        logs = logs + eliminate(s_ref, t_ref)
        inv_ref[pl.ds(at, B), :] = t_ref[...]
        for own in range(blocks - 1):
            lo = (own + 1) * B
            here = slice(own * B, lo)

            @pl.when(j == own)
            def _():
                inverse = split(t_ref[...])

                @pl.loop(own + 1, blocks)
                def _(r):
                    rows = pl.ds(pl.multiple_of(r * B, B), B)
                    high, low = split(three(one_nt, split(l_ref[rows, here]), inverse))
                    hi_ref[rows, here] = high
                    lo_ref[rows, here] = low

                for first in range(lo, points, 2 * B):
                    last = min(first + 2 * B, points)

                    @pl.loop(first // B, blocks)
                    def _(r):
                        rows = pl.ds(pl.multiple_of(r * B, B), B)
                        l_ref[rows, first:last] = l_ref[rows, first:last] - three(
                            one_nt,
                            (hi_ref[rows, here], lo_ref[rows, here]),
                            (hi_ref[first:last, here], lo_ref[first:last, here]),
                        )

        return logs

    logs = lax.fori_loop(0, blocks, panel, jnp.zeros((T, B), jnp.float32))
    log_ref[...] = jnp.broadcast_to(jnp.sum(logs, axis=0, keepdims=True), (T, B))


def leaf_kernel(
    a_ref, r_ref, order_ref, hi_ref, lo_ref, inv_ref, log_ref, xh_ref, xl_ref, xr_ref, diag_ref, red_ref, x_ref
):
    width, points = a_ref.shape
    count = r_ref.shape[0]
    total = width + count
    sensor = lax.broadcasted_iota(jnp.int32, (points, B), 0)
    cut = pieces(r_ref[...])
    for lo in range(0, points, B):
        pick = jnp.where(sensor == order_ref[0:1, lo : lo + B], 1.0, 0.0).astype(jnp.bfloat16)
        part = one_nn(cut, pick)
        x_ref[width:, lo : lo + B] = (
            part[:count] + part[count : 2 * count] + part[2 * count :]
        )
        x_ref[:width, lo : lo + B] = a_ref[:, lo : lo + B]
    step = total // 5
    for lo in range(0, points, 2 * B):
        middle, hi = lo + B, lo + 2 * B
        first = split(inv_ref[lo:middle, :])
        second = split(inv_ref[middle:hi, :])

        @pl.loop(0, 5)
        def _(r):
            rows = pl.ds(pl.multiple_of(r * step, 2 * T), step)
            value = x_ref[rows, lo:hi]
            if lo > 0:
                value = value - three(
                    one_nt,
                    (xh_ref[rows, :lo], xl_ref[rows, :lo]),
                    (hi_ref[lo:hi, :lo], lo_ref[lo:hi, :lo]),
                )
            solved = three(one_nt, split(value[:, :B]), first)
            x_ref[rows, lo:middle] = solved
            high, low = split(solved)
            xh_ref[rows, lo:middle] = high
            xl_ref[rows, lo:middle] = low
            rest = value[:, B:] - three(
                one_nt, (high, low), (hi_ref[middle:hi, lo:middle], lo_ref[middle:hi, lo:middle])
            )
            solved = three(one_nt, split(rest), second)
            x_ref[rows, middle:hi] = solved
            high, low = split(solved)
            xh_ref[rows, middle:hi] = high
            xl_ref[rows, middle:hi] = low

    xr_ref[...] = x_ref[width:, :]
    starts = columns(width // B, count)
    for j in range(0, width // B, 2):
        lo, middle, hi = j * B, (j + 1) * B, (j + 2) * B
        right = (xh_ref[lo:hi, :], xl_ref[lo:hi, :])

        def put(rows, at, size, both):
            value = three(one_nt, (xh_ref[rows, :], xl_ref[rows, :]), right)
            if j == 0 and not both:
                diag_ref[...] = value[:, :B]
            else:
                red_ref[pl.ds(starts[j] + at, size), :] = value[:, :B]
            if both:
                red_ref[pl.ds(starts[j + 1] + at - B, size), :] = value[:, B:]

        put(slice(lo, middle), 0, B, False)

        @pl.loop(j + 1, width // B)
        def _(r):
            put(pl.ds(pl.multiple_of(r * B, B), B), pl.multiple_of((r - j) * B, B), B, True)

        put(slice(width, total), width - lo, count, True)
    lane = lax.broadcasted_iota(jnp.int32, (TAIL, B), 1)
    red_ref[starts[-1] :, :] = jnp.where(lane == 0, log_ref[0:1, :], 0.0)


def pivot_kernel(own_ref, other_ref, inv_ref, log_ref, s_ref):
    rows = lax.broadcasted_iota(jnp.int32, (B, B), 0)
    lanes = lax.broadcasted_iota(jnp.int32, (B, B), 1)
    eye = jnp.where(rows == lanes, 1.0, 0.0).astype(jnp.float32)
    s_ref[...] = eye + (own_ref[...] + other_ref[...])
    logs = eliminate(s_ref, inv_ref)
    log_ref[...] = jnp.broadcast_to(jnp.sum(logs, axis=0, keepdims=True), (T, B))


def head_kernel(blocks, count, halved, core_ref, own_ref, *refs):
    others, refs = refs[: 2 if halved else 1], refs[2 if halved else 1 :]
    inv_ref, y_ref, diag_ref, sum_ref = refs
    starts = columns(blocks, count)
    if halved:
        first = core_ref[0, 0] == 0
        half = own_ref.shape[0] // 2
        near, far = others[0][...], others[1][...]
        sum_ref[:half, :] = own_ref[:half, :] + jnp.where(first, near, far)
        sum_ref[half:, :] = own_ref[half:, :] + jnp.where(first, far, near)
    else:
        sum_ref[...] = own_ref[...] + others[0][...]
    y_ref[...] = dot_nt(sum_ref[: starts[1], :], inv_ref[...])
    if blocks > 1:
        at = starts[1]
        diag_ref[...] = sum_ref[at : at + B, :] - dot_nt(y_ref[:B, :], y_ref[:B, :])
    else:
        diag_ref[...] = jnp.zeros((B, B), jnp.float32)


def rest_kernel(depth, blocks, count, core_ref, sum_ref, y_ref, log_ref, out_ref, *half_refs):
    starts = columns(blocks, count)
    after = columns(blocks - 1, count)
    lane = lax.broadcasted_iota(jnp.int32, (TAIL, B), 1)
    out_ref[after[-1] :, :] = jnp.where(
        lane == depth + 1, log_ref[0:1, :], sum_ref[starts[-1] :, :]
    )
    for j in range(blocks - 1):
        skip = B if j == 0 else 0
        out_ref[after[j] + skip : after[j + 1], :] = sum_ref[
            starts[j + 1] + skip : starts[j + 2], :
        ] - dot_nt(y_ref[j * B + skip :, :], y_ref[j * B : (j + 1) * B, :])
    if half_refs:
        half = half_refs[0].shape[0]
        first = core_ref[0, 0] == 0
        half_refs[0][...] = jnp.where(first, out_ref[:half, :], out_ref[half:, :])


def back_kernel(levels, *refs):
    invs = refs[:levels]
    ys = refs[levels : 2 * levels]
    xh_ref, xl_ref, xr_ref, hi_ref, lo_ref, inv_ref, order_ref, out_ref, c_ref, z_ref = refs[
        2 * levels :
    ]
    count, points = out_ref.shape
    width = levels * B
    for depth in reversed(range(levels)):
        left = (levels - depth - 1) * B
        target = ys[depth][left:, :]
        lo = depth * B
        if left > 0:
            target = target - dot_nn(c_ref[:, lo + B :], ys[depth][:left, :])
        c_ref[:, lo : lo + B] = dot_nn(target, invs[depth][...])
    coefficients = split(c_ref[...])
    for lo in range(0, points, 2 * B):
        here = slice(lo, lo + 2 * B)
        z_ref[:, here] = xr_ref[:, here] - three(
            one_nn, coefficients, (xh_ref[:width, here], xl_ref[:width, here])
        )
    for lo in reversed(range(0, points, B)):
        hi = lo + B
        value = z_ref[:, lo:hi]
        if hi < points:
            value = value - three(
                one_nn, split(z_ref[:, hi:]), (hi_ref[hi:, lo:hi], lo_ref[hi:, lo:hi])
            )
        z_ref[:, lo:hi] = three(one_nn, split(value), split(inv_ref[lo:hi, :]))
    sensor = lax.broadcasted_iota(jnp.int32, (points, 2 * B), 0)
    for lo in range(0, points, 2 * B):
        hi = lo + 2 * B
        pick = jnp.where(sensor == order_ref[0:1, lo:hi], 1.0, 0.0).astype(jnp.bfloat16)
        part = one_nt(pieces(z_ref[:, lo:hi]), pick)
        part = part[:count] + part[count : 2 * count] + part[2 * count :]
        out_ref[...] = part if lo == 0 else out_ref[...] + part


def call(kernel, name, outs, scratch, *operands, smem=0, work=None, limit=48):
    typed = [out if isinstance(out[0], tuple) else (out, jnp.float32) for out in outs]
    return pl.pallas_call(
        kernel,
        name=name,
        out_shape=[jax.ShapeDtypeStruct(*out) for out in typed],
        in_specs=[pl.BlockSpec(memory_space=pltpu.SMEM)] * smem
        + [pl.BlockSpec(memory_space=pltpu.VMEM)] * (len(operands) - smem),
        out_specs=[pl.BlockSpec(memory_space=pltpu.VMEM)] * len(outs),
        scratch_shapes=[pltpu.VMEM(shape, jnp.float32) for shape in scratch],
        compiler_params=pltpu.CompilerParams(vmem_limit_bytes=limit * 2**20),
        cost_estimate=work,
    )(*operands)


def shards(leaf_blocks, generators, rhs, order, ranks):
    levels, quarter, points = generators.shape
    count = rhs.shape[0]
    replica = lax.axis_index("rep")
    rank_index = lax.broadcasted_iota(jnp.int32, (levels, quarter, 1), 1) + replica * quarter
    masked = jnp.where(rank_index < ranks[:, :, None], generators, 0.0)
    gathered = lax.all_gather(masked, "rep", axis=1, tiled=True)
    width = levels * B
    stacked = gathered.reshape(width, points)
    square = [(B, B), (B, B)]
    narrow = ((points, points), jnp.bfloat16)
    high, low, inverse, logs = call(
        factor_kernel,
        "leaf_factor",
        [narrow, narrow, (points, B), (T, B)],
        [(points, points)] + square,
        leaf_blocks,
    )
    narrow = ((width + count, points), jnp.bfloat16)
    half_high, half_low, half_right, diagonal, reduced = call(
        leaf_kernel,
        "leaf_reduce",
        [narrow, narrow, (count, points), (B, B), (packed(levels, count), B)],
        [(width + count, points)],
        stacked,
        rhs,
        order,
        high,
        low,
        inverse,
        logs,
    )
    invs, ys = [], []
    core = (lax.axis_index("leaf") % 2).astype(jnp.int32).reshape(1, 1)
    work = pl.CostEstimate(flops=2**22, bytes_accessed=2**24, transcendentals=0)
    short = pl.CostEstimate(flops=2**22, bytes_accessed=2**22, transcendentals=0)
    part = None
    for depth in range(levels):
        blocks = levels - depth
        left = (blocks - 1) * B
        halved = depth in HALVED
        other = swapped(diagonal, "leaf", depth)
        sent = part if halved else reduced
        if depth < levels - 1:
            sent, other = lax.optimization_barrier((sent, other))
        near = swapped(sent, "leaf", depth)
        pivot_inverse, logs = call(
            pivot_kernel, "pivot", [(B, B), (T, B)], [(B, B)], diagonal, other, work=work, limit=12
        )
        received = [near]
        if halved:
            near, pivot_inverse = lax.optimization_barrier((near, pivot_inverse))
            received = [near, swapped(near, "leaf", 0)]
        pivot_right, diagonal, sums = call(
            functools.partial(head_kernel, blocks, count, halved),
            "head_%d" % depth,
            [(left + count, B), (B, B), (packed(blocks, count), B)],
            [],
            core,
            reduced,
            *received,
            pivot_inverse,
            smem=1,
            work=short,
            limit=12,
        )
        following = packed(blocks - 1, count)
        halving = depth + 1 in HALVED and depth + 1 < levels
        reduced, *parts = call(
            functools.partial(rest_kernel, depth, blocks, count),
            "rest_%d" % depth,
            [(following, B)] + [(following // 2, B)] * halving,
            [],
            core,
            sums,
            pivot_right,
            logs,
            smem=1,
            work=short,
            limit=12,
        )
        part = parts[0] if halving else None
        invs.append(pivot_inverse)
        ys.append(pivot_right)
    leaf_count = lax.axis_size("leaf")
    terms = [leaf_count * points] + [leaf_count // 2 ** (depth + 1) * B for depth in range(levels)]
    determinants = reduced[0, : levels + 1] / jnp.array(terms, jnp.float32)
    (solution,) = call(
        functools.partial(back_kernel, levels),
        "back_solve",
        [(count, points)],
        [(count, width), (count, points)],
        *invs,
        *ys,
        half_high,
        half_low,
        half_right,
        high,
        low,
        inverse,
        order,
        limit=24,
    )
    return (solution, determinants)


def solution(mesh):
    placed = (
        P("leaf", None),
        P(None, "rep", "leaf"),
        P("rep", "leaf"),
        P("leaf", None),
        P(None, "leaf"),
    )
    return jax.shard_map(
        shards, mesh=mesh, in_specs=placed, out_specs=(P("rep", "leaf"), P()), check_vma=False
    )
```
